32 devices in a mesh: dev: 32 (over z, y, x, core).
Axes of the slice: x: 2, y: 2, z: 4, core: 2. Of those that a mesh axis runs over, the one named last changes fastest.
Arguments:
- prior_labels: bfloat16 [65536, 512], P('dev'), may hold values from 0.0009994507 to 1
- label_class: int32 [65536], P('dev'), may hold values from 0 to 511
- labeled: int32 [65536], P('dev'), may hold values 0 or 1
- features: bfloat16 [65536, 1024], P('dev'), may hold values from -6 to 6
- tile_cols: int32 [512, 8], P('dev'), may hold values from 0 to 17, as said below
- tile_weights: bfloat16 [512, 8, 128, 128], P('dev'), may hold values from 0 to 1, as said below
- halo_owner: int32 [8192, 1], P('dev'), may hold values from 0 to 31; in each aligned block of 256 rows (0 to 255, 256 to 511, ...) at most 16 rows name the same one
- halo_local: int32 [8192], P('dev'), may hold values from 0 to 2047
- batch_owner: int32 [16384, 1], P('dev'), may hold values from 0 to 31; in each aligned block of 512 rows (0 to 511, 512 to 1023, ...) at most 32 rows name the same one
- batch_local: int32 [16384], P('dev'), may hold values from 0 to 2047
- w_in: bfloat16 [4096, 1024], replicated, may hold values from -0.1875 to 0.1875
- w_out: bfloat16 [4096, 512], replicated, may hold values from -0.09375 to 0.09375
Outputs:
- propagated: bfloat16 [65536, 512], P('dev')
- row_error: float32 [16384], P('dev')
- grad_in: float32 [4096, 1024], P('dev')
- grad_out: float32 [4096, 512], P('dev')
The draws below stay inside these ranges and needn't reach their ends.
Inputs may be any that keep to these rules, and one draw needn't show every extreme that they name: `tile_cols`: in each row tile's list the first 6 entries are tiles of the device's own rows (below 16), the first of them the row tile itself; the last 2 are halo tiles (16 and above). Entries may repeat. Every halo tile of a device is listed by some row tile of that device. `tile_weights`: strictly positive. `halo_owner`: within the 256 rows of one device no owner appears more than 16 times; in some device one owner appears exactly 16 times. `batch_owner`: within the 512 rows of one device no owner appears more than 32 times; in some device one owner appears exactly 32 times.
All inputs are finite; a program needn't handle non-finite values. No bound on the sum of `labeled` on one device may be relied on, other than what follows from the above.
Results may differ from the reference program's by a relative error of at most 0.0017.
Values may be sent and summed in bfloat16 or wider, within the bound.
A program may use at most 128 MiB of HBM per device.

```python
import math
import jax
import jax.numpy as jnp
import numpy as np
from jax import lax

TILE = 128
CLASSES = 512
FEAT = 1024
HID = 4096
TPR_LOCAL = 6
TPR_HALO = 2
NODE_DEV = 2048
HALO_DEV = 256
BATCH_DEV = 512
TPR = 8
CAPR = 16
CAPB = 32
NODES = 65536
HALO = 8192
BATCH = 16384
N_DEV = 32


def draw_tile_cols(key, part):
    row_tiles = NODES // TILE
    own_count = NODE_DEV // TILE
    halo_count = HALO_DEV // TILE
    first_key, second_key = jax.random.split(jax.random.fold_in(key, 17))
    itself = jnp.arange(row_tiles, dtype=jnp.int32) % own_count
    nearby = jax.random.randint(first_key, (row_tiles, TPR_LOCAL - 1), 0, own_count, dtype=jnp.int32)
    covering = itself % halo_count + own_count
    remote = jax.random.randint(second_key, (row_tiles, TPR_HALO - 1), 0, halo_count, dtype=jnp.int32) + own_count
    return jnp.concatenate([itself[:, None], nearby, covering[:, None], remote], axis=1)


def draw_tile_weights(key, part):
    normal = jnp.clip(jax.random.normal(jax.random.fold_in(key, 29), (NODES // TILE, TPR, TILE, TILE), dtype=jnp.float32), -3.0, 3.0)
    spread = 2.0
    return jnp.exp(spread * (normal - 3.0)).astype(jnp.bfloat16)


def plant(entries, rng, low, largest):
    spot = [jax.random.randint(jax.random.fold_in(rng, axis), (), 0, length) for axis, length in enumerate(entries.shape)]
    longest = entries.shape.index(max(entries.shape))
    neighbour = spot[:longest] + [(spot[longest] + 1) % entries.shape[longest]] + spot[longest + 1:]
    return entries.at[tuple(spot)].set(low).at[tuple(neighbour)].set(largest)


def level_of(own_key, dims, pieces, least, high):
    gain = 1.0
    for dim, blocks in pieces:
        heights = jax.random.uniform(jax.random.fold_in(jax.random.fold_in(own_key, 6), dim), (blocks,), jnp.float32, least / len(pieces), high / len(pieces))
        gain = gain * jnp.repeat(jnp.exp(heights), dims[dim] // blocks).reshape((-1,) + (1,) * (len(dims) - 1 - dim))
    return gain


def assign_block(rng, own, number, rows, count, top, limit, slope):
    ranking = jax.random.permutation(rng, count)
    packed, usual = load_shares(count, rows * top, limit, slope, True), load_shares(count, rows * top, limit, slope, False)
    places = jnp.arange(count)

    def named(sizes, rotation):
        used = int((sizes > 0).sum())
        fixed = max(1, used // 4)
        moved = fixed + (places - fixed + rotation * (used - fixed)) % max(1, count - fixed)
        return jnp.zeros((count,), jnp.int32).at[ranking[jnp.where(places < fixed, places, moved)]].set(jnp.asarray(sizes, jnp.int32))

    sizes = jnp.where(number % 4 == 0, named(packed, number // 4), named(usual, number - number // 4 - 1))
    mixed = jax.random.permutation(jax.random.fold_in(own, 3), count)
    source_of, taker = mixed[0:count // 2 * 2:2], mixed[1:count // 2 * 2:2]
    slack = jnp.minimum(sizes[source_of] - 1, limit - sizes[taker]) // 2
    slack = jnp.where((source_of == ranking[0]) | (taker == ranking[0]) | (sizes[taker] == 0), 0, jnp.maximum(slack, 0))
    moved = jax.random.randint(jax.random.fold_in(own, 4), (count // 2,), 0, 1 << 20) % (slack + 1)
    sizes = sizes.at[source_of].add(-moved).at[taker].add(moved)
    labels = jnp.searchsorted(jnp.cumsum(sizes), jnp.arange(rows * top), side="right").astype(jnp.int32)
    table = labels.reshape(top, rows).T
    table = table[jax.random.permutation(jax.random.fold_in(own, 1), rows)]
    rotation = jax.random.randint(jax.random.fold_in(own, 2), (rows, 1), 0, top)
    return jnp.take_along_axis(table, (jnp.arange(top)[None, :] + rotation) % top, axis=1)


def load_shares(number_of, total, limit, skew, full):
    weights = [(1 << 20) // math.isqrt(standing ** skew) + 1 for standing in range(1, number_of + 1)]
    largest = limit if full else min(limit, max(-(-total // number_of), total * weights[0] // sum(weights)))
    least = 1 if total - largest >= number_of - 1 else 0
    holding, spare = [largest] + [least] * (number_of - 1), total - largest - least * (number_of - 1)
    while spare > 0:
        movable = [i for i in range(1, number_of) if holding[i] < largest] or [i for i in range(1, number_of) if holding[i] < limit]
        whole, left = sum([weights[i] for i in movable]), spare
        for i in movable:
            more = min(limit - holding[i], max(1, left * weights[i] // whole), spare)
            holding[i] = holding[i] + more
            spare = spare - more
    return np.array(holding)


def noise(rng, shape, width, limit, cuts=(), held_as=jnp.bfloat16):
    level = level_of(rng, shape, cuts, -0.22, 0.18) if cuts else 1.0
    drawn = jax.random.normal(rng, shape, jnp.float32) * width * level
    return jnp.minimum(jnp.maximum(drawn, -limit), limit).astype(held_as)


def setup_inputs(seed: int = 0) -> dict:
    key_of = jax.random.split(jax.random.key(seed), 13)
    prior_labels = jnp.clip(jnp.exp(math.log(1.0) - 6.9083047 * jax.random.uniform(key_of[0], (NODES, CLASSES), jnp.float32) ** level_of(key_of[0], (NODES, CLASSES), ((0, 32),), -0.2, 0.2)), 0.0009994507, 1.0).astype(jnp.bfloat16)
    label_class = plant(jax.random.randint(key_of[1], (NODES,), 0, CLASSES), jax.random.fold_in(key_of[1], 1), 0, CLASSES - 1).astype(jnp.int32)
    labeled = plant((jax.random.randint(key_of[2], (NODES,), 0, 4) < 1).astype(jnp.int32), jax.random.fold_in(key_of[2], 1), 0, 1)
    features = noise(key_of[3], (NODES, FEAT), 1.0, 6.0, ((0, 32),))
    tile_cols = draw_tile_cols(jax.random.fold_in(key_of[12], 71), 0)
    tile_weights = draw_tile_weights(jax.random.fold_in(key_of[12], 71), 0)
    halo_owner_keys = jax.random.split(jax.random.fold_in(key_of[6], 1), HALO // HALO_DEV)
    halo_owner_turns = jax.random.permutation(jax.random.fold_in(key_of[6], 3), HALO // HALO_DEV)
    halo_owner = jax.vmap(lambda own, number: assign_block(jax.random.fold_in(key_of[6], 2), own, number, HALO_DEV, N_DEV, 1, CAPR, 1))(halo_owner_keys, halo_owner_turns).reshape((HALO, 1))
    halo_local = plant(jax.random.randint(key_of[7], (HALO,), 0, NODE_DEV), jax.random.fold_in(key_of[7], 1), 0, NODE_DEV - 1).astype(jnp.int32)
    batch_owner_keys = jax.random.split(jax.random.fold_in(key_of[8], 1), BATCH // BATCH_DEV)
    batch_owner_turns = jax.random.permutation(jax.random.fold_in(key_of[8], 3), BATCH // BATCH_DEV)
    batch_owner = jax.vmap(lambda own, number: assign_block(jax.random.fold_in(key_of[8], 2), own, number, BATCH_DEV, N_DEV, 1, CAPB, 1))(batch_owner_keys, batch_owner_turns).reshape((BATCH, 1))
    batch_local = plant(jax.random.randint(key_of[9], (BATCH,), 0, NODE_DEV), jax.random.fold_in(key_of[9], 1), 0, NODE_DEV - 1).astype(jnp.int32)
    w_in = noise(key_of[10], (HID, FEAT), FEAT ** -0.5, 0.1875)
    w_out = noise(key_of[11], (HID, CLASSES), HID ** -0.5, 0.09375)
    return {"prior_labels": prior_labels, "label_class": label_class, "labeled": labeled, "features": features, "tile_cols": tile_cols, "tile_weights": tile_weights, "halo_owner": halo_owner, "halo_local": halo_local, "batch_owner": batch_owner, "batch_local": batch_local, "w_in": w_in, "w_out": w_out}


def reference(prior_labels, label_class, labeled, features, tile_cols, tile_weights, halo_owner, halo_local, batch_owner, batch_local, w_in, w_out):
    devices = N_DEV
    own_tiles = NODE_DEV // TILE
    halo_tiles = HALO_DEV // TILE
    halo_node = (halo_owner[:, 0] * NODE_DEV + halo_local).astype(jnp.int32)
    halo_labels = prior_labels[halo_node]
    table = jnp.concatenate([prior_labels.reshape(devices, own_tiles, TILE, CLASSES), halo_labels.reshape(devices, halo_tiles, TILE, CLASSES)], axis=1)
    columns = tile_cols.reshape(devices, own_tiles, TPR)
    weights = tile_weights.reshape(devices, own_tiles, TPR, TILE, TILE)
    given_class = label_class.reshape(devices, NODE_DEV)
    marked = labeled.reshape(devices, NODE_DEV)

    def one_device(inputs):
        block_table, block_cols, block_weights, block_class, block_mark = inputs
        blocks = block_table[block_cols].astype(jnp.float32)
        wide_weights = block_weights.astype(jnp.float32)
        spread = jnp.einsum('rkij,rkjc->ric', wide_weights, blocks, precision=lax.Precision.HIGHEST)
        degree = lax.optimization_barrier(jnp.sum(wide_weights, axis=(1, 3)))
        seeds = ((block_class[:, None] == jnp.arange(CLASSES, dtype=jnp.int32)[None, :]) & (block_mark[:, None] == 1)).astype(jnp.float32)
        mixed = 0.8 * (spread / degree[:, :, None]).reshape(NODE_DEV, CLASSES) + 0.2 * seeds
        return mixed.astype(jnp.bfloat16)
    propagated = lax.map(one_device, (table, columns, weights, given_class, marked)).reshape(NODES, CLASSES)
    batch_node = (batch_owner[:, 0] * NODE_DEV + batch_local).astype(jnp.int32)
    batch_x = features[batch_node]
    batch_z = propagated[batch_node]
    log_z = jnp.log(batch_z.astype(jnp.float32))
    target = log_z - lax.optimization_barrier(jnp.mean(log_z, axis=1, keepdims=True))
    hidden = jnp.tanh(jnp.dot(batch_x, w_in.T, preferred_element_type=jnp.float32)).astype(jnp.bfloat16)
    logits = jnp.dot(hidden, w_out, preferred_element_type=jnp.float32)
    differ = logits - target
    row_error = 0.5 * lax.optimization_barrier(jnp.mean(differ * differ, axis=1))
    residue = (differ / math.sqrt(BATCH)).astype(jnp.bfloat16)
    grad_out = jnp.dot(hidden.T, residue, preferred_element_type=jnp.float32)
    hidden_wide = hidden.astype(jnp.float32)
    back = (jnp.dot(residue, w_out.T, preferred_element_type=jnp.float32) * (1.0 - hidden_wide * hidden_wide)).astype(jnp.bfloat16)
    grad_in = jnp.dot(back.T, batch_x, preferred_element_type=jnp.float32)
    return (propagated, row_error, grad_in, grad_out)
```

```python
import math

import jax
import jax.numpy as jnp
from jax import lax
from jax.experimental import pallas as pl
from jax.experimental.pallas import tpu as pltpu
from jax.sharding import PartitionSpec as P


def slot_of(owner, capacity):
    row = jnp.arange(owner.shape[0], dtype=jnp.int32)
    same = (owner[:, None] == owner[None, :]) & (row[None, :] < row[:, None])
    return owner * capacity + jnp.sum(same.astype(jnp.int32), axis=1)


def request_table(position, local, capacity, devices):
    slot = jnp.arange(devices * capacity, dtype=jnp.int32)
    match = slot[:, None] == position[None, :]
    table = jnp.sum(jnp.where(match, local[None, :] + 1, 0), axis=1) - 1
    return table.reshape(devices, capacity)


def contract_rows(left, right):
    return lax.dot_general(
        left, right, (((0,), (0,)), ((), ())), preferred_element_type=jnp.float32
    )


def contract_cols(left, right):
    return lax.dot_general(
        left, right, (((1,), (1,)), ((), ())), preferred_element_type=jnp.float32
    )


def spread_kernel(cols_ref, weights_ref, own_ref, halo_ref, seed_ref, out_ref, table_ref):
    r = pl.program_id(0)
    per_row = weights_ref.shape[1]
    rows = weights_ref.shape[2]
    own = own_ref.shape[0]

    @pl.when(r == 0)
    def _():
        table_ref[:own] = own_ref[...]
        table_ref[own:] = halo_ref[...]

    total = jnp.zeros((rows, own_ref.shape[2]), jnp.float32)
    weight = jnp.zeros((rows, weights_ref.shape[3]), jnp.float32)
    for k in range(per_row):
        block = weights_ref[0, k]
        total += jnp.dot(block, table_ref[cols_ref[r, k]], preferred_element_type=jnp.float32)
        weight += block.astype(jnp.float32)
    degree = jnp.sum(weight, axis=1, keepdims=True)
    classes = lax.broadcasted_iota(jnp.int32, total.shape, 1)
    seeds = (classes == seed_ref[...]).astype(jnp.float32)
    out_ref[...] = (0.8 * (total / degree) + 0.2 * seeds).astype(out_ref.dtype)


def propagate(tile_cols, tile_weights, prior_labels, halo_labels, seed_class):
    row_tiles, per_row, rows, _ = tile_weights.shape
    node_count, classes = prior_labels.shape
    own_tiles = node_count // rows
    halo_tiles = halo_labels.shape[0] // rows
    return pl.pallas_call(
        spread_kernel,
        out_shape=jax.ShapeDtypeStruct((node_count, classes), jnp.bfloat16),
        grid_spec=pltpu.PrefetchScalarGridSpec(
            num_scalar_prefetch=1,
            grid=(row_tiles,),
            in_specs=[
                pl.BlockSpec((1, per_row, rows, rows), lambda r, c: (r, 0, 0, 0)),
                pl.BlockSpec((own_tiles, rows, classes), lambda r, c: (0, 0, 0)),
                pl.BlockSpec((halo_tiles, rows, classes), lambda r, c: (0, 0, 0)),
                pl.BlockSpec((rows, 1), lambda r, c: (r, 0)),
            ],
            out_specs=pl.BlockSpec((rows, classes), lambda r, c: (r, 0)),
            scratch_shapes=[pltpu.VMEM((own_tiles + halo_tiles, rows, classes), jnp.bfloat16)],
        ),
        compiler_params=pltpu.CompilerParams(
            dimension_semantics=("arbitrary",), vmem_limit_bytes=24 << 20
        ),
        cost_estimate=pl.CostEstimate(
            flops=2 * node_count * per_row * rows * classes,
            bytes_accessed=2 * (tile_weights.size + 2 * prior_labels.size),
            transcendentals=0,
        ),
    )(
        tile_cols,
        tile_weights,
        prior_labels.reshape(own_tiles, rows, classes),
        halo_labels.reshape(halo_tiles, rows, classes),
        seed_class[:, None],
    )


def on_device(
    prior_labels,
    label_class,
    labeled,
    features,
    tile_cols,
    tile_weights,
    halo_owner,
    halo_local,
    batch_owner,
    batch_local,
    w_in,
    w_out,
):
    devices = lax.axis_size("dev")
    chips = devices // 2
    me = lax.axis_index("dev")
    chip, core = me // 2, lax.rem(me, 2)
    swap = [(i, i ^ 1) for i in range(devices)]
    across = [[2 * i + c for i in range(chips)] for c in range(2)]

    classes = prior_labels.shape[1]
    feat_width = features.shape[1]
    hidden_units = w_in.shape[0]
    unit_block = hidden_units // devices
    halo_count = halo_owner.shape[0]
    batch_count = batch_owner.shape[0]
    halo_capacity = 2 * halo_count // devices
    batch_capacity = 2 * batch_count // devices
    slots = devices * batch_capacity

    halo_slot = slot_of(halo_owner[:, 0], halo_capacity)
    batch_slot = slot_of(batch_owner[:, 0], batch_capacity)
    asked = jnp.concatenate(
        [
            request_table(halo_slot, halo_local, halo_capacity, devices),
            request_table(batch_slot, batch_local, batch_capacity, devices),
        ],
        axis=1,
    )
    wanted = lax.all_to_all(asked, "dev", split_axis=0, concat_axis=0, tiled=True)
    halo_wanted = jnp.maximum(wanted[:, :halo_capacity], 0).reshape(-1)
    batch_asked = wanted[:, halo_capacity:].reshape(-1)
    batch_wanted = jnp.maximum(batch_asked, 0)
    halo_back = lax.all_to_all(
        prior_labels[halo_wanted].reshape(devices, halo_capacity, classes),
        "dev",
        split_axis=0,
        concat_axis=0,
        tiled=True,
    )

    w_in_half = lax.dynamic_index_in_dim(
        w_in.reshape(chips, 2, unit_block, feat_width), core, 1, keepdims=False
    ).reshape(-1, feat_width)
    w_out_half = lax.dynamic_index_in_dim(
        w_out.reshape(chips, 2, unit_block, classes), core, 1, keepdims=False
    ).reshape(-1, classes)

    def both_cores(own):
        return jnp.concatenate([own, lax.ppermute(own, "dev", swap)], axis=0)

    x = both_cores(features[batch_wanted])
    hidden = jnp.tanh(contract_cols(x, w_in_half)).astype(jnp.bfloat16)
    partial = jnp.dot(hidden, w_out_half, preferred_element_type=jnp.float32)
    logits = partial[:slots] + lax.ppermute(partial[slots:], "dev", swap)

    halo_labels = halo_back.reshape(devices * halo_capacity, classes)[halo_slot]
    seed_class = jnp.where(labeled == 1, label_class, -1)
    propagated = propagate(tile_cols, tile_weights, prior_labels, halo_labels, seed_class)

    log_z = jnp.log(propagated[batch_wanted].astype(jnp.float32))
    target = log_z - jnp.mean(log_z, axis=1, keepdims=True)
    differ = logits - target
    slot_error = 0.5 * jnp.mean(differ * differ, axis=1)
    scaled = differ / math.sqrt(batch_count * devices)
    residue_own = jnp.where((batch_asked >= 0)[:, None], scaled, 0.0).astype(jnp.bfloat16)
    residue = both_cores(residue_own)

    def over_chips(left, right):
        gradient = contract_rows(left, right).astype(jnp.bfloat16)
        own = contract_rows(lax.dynamic_slice_in_dim(left, chip * unit_block, unit_block, 1), right)
        blocks = lax.all_to_all(
            gradient.reshape(chips, unit_block, gradient.shape[1]),
            "dev",
            split_axis=0,
            concat_axis=0,
            tiled=True,
            axis_index_groups=across,
        )
        other = (jnp.arange(chips, dtype=jnp.int32) != chip)[:, None, None]
        return own + jnp.sum(jnp.where(other, blocks.astype(jnp.float32), 0.0), axis=0)

    grad_out = over_chips(hidden, residue)
    hidden_wide = hidden.astype(jnp.float32)
    back = (contract_cols(residue, w_out_half) * (1.0 - hidden_wide * hidden_wide)).astype(
        jnp.bfloat16
    )
    grad_in = over_chips(back, x)

    error_back = lax.all_to_all(
        slot_error.reshape(devices, batch_capacity),
        "dev",
        split_axis=0,
        concat_axis=0,
        tiled=True,
    ).reshape(-1)
    mine = batch_slot[:, None] == jnp.arange(slots, dtype=jnp.int32)[None, :]
    row_error = jnp.sum(jnp.where(mine, error_back[None, :], 0.0), axis=1)
    return (propagated, row_error, grad_in, grad_out)


def solution(mesh):
    in_specs = (
        P("dev", None),
        P("dev"),
        P("dev"),
        P("dev", None),
        P("dev", None),
        P("dev", None, None, None),
        P("dev", None),
        P("dev"),
        P("dev", None),
        P("dev"),
        P(),
        P(),
    )
    out_specs = (P("dev", None), P("dev"), P("dev", None), P("dev", None))
    return jax.shard_map(
        on_device, mesh=mesh, in_specs=in_specs, out_specs=out_specs, check_vma=False
    )
```

```python
import math

import jax
import jax.numpy as jnp
from jax import lax
from jax.experimental import pallas as pl
from jax.experimental.pallas import tpu as pltpu
from jax.sharding import PartitionSpec as P


def slot_of(owner, capacity):
    row = jnp.arange(owner.shape[0], dtype=jnp.int32)
    same = (owner[:, None] == owner[None, :]) & (row[None, :] < row[:, None])
    return owner * capacity + jnp.sum(same.astype(jnp.int32), axis=1)


def request_table(position, local, capacity, devices):
    slot = jnp.arange(devices * capacity, dtype=jnp.int32)
    match = slot[:, None] == position[None, :]
    table = jnp.sum(jnp.where(match, local[None, :] + 1, 0), axis=1) - 1
    return table.reshape(devices, capacity)


def contract_rows(left, right):
    return lax.dot_general(
        left, right, (((0,), (0,)), ((), ())), preferred_element_type=jnp.float32
    )


def contract_cols(left, right):
    return lax.dot_general(
        left, right, (((1,), (1,)), ((), ())), preferred_element_type=jnp.float32
    )


def spread_kernel(cols_ref, weights_ref, own_ref, halo_ref, seed_ref, out_ref, table_ref):
    r = pl.program_id(0)
    per_row = weights_ref.shape[1]
    rows = weights_ref.shape[2]
    own = own_ref.shape[0]

    @pl.when(r == 0)
    def _():
        table_ref[:own] = own_ref[...]
        table_ref[own:] = halo_ref[...]

    total = jnp.zeros((rows, own_ref.shape[2]), jnp.float32)
    weight = jnp.zeros((rows, weights_ref.shape[3]), jnp.float32)
    for k in range(per_row):
        block = weights_ref[0, k]
        total += jnp.dot(block, table_ref[cols_ref[r, k]], preferred_element_type=jnp.float32)
        weight += block.astype(jnp.float32)
    degree = jnp.sum(weight, axis=1, keepdims=True)
    classes = lax.broadcasted_iota(jnp.int32, total.shape, 1)
    seeds = (classes == seed_ref[...]).astype(jnp.float32)
    out_ref[...] = (0.8 * (total / degree) + 0.2 * seeds).astype(out_ref.dtype)


def propagate(tile_cols, tile_weights, prior_labels, halo_labels, seed_class):
    row_tiles, per_row, rows, _ = tile_weights.shape
    node_count, classes = prior_labels.shape
    own_tiles = node_count // rows
    halo_tiles = halo_labels.shape[0] // rows
    return pl.pallas_call(
        spread_kernel,
        out_shape=jax.ShapeDtypeStruct((node_count, classes), jnp.bfloat16),
        grid_spec=pltpu.PrefetchScalarGridSpec(
            num_scalar_prefetch=1,
            grid=(row_tiles,),
            in_specs=[
                pl.BlockSpec((1, per_row, rows, rows), lambda r, c: (r, 0, 0, 0)),
                pl.BlockSpec((own_tiles, rows, classes), lambda r, c: (0, 0, 0)),
                pl.BlockSpec((halo_tiles, rows, classes), lambda r, c: (0, 0, 0)),
                pl.BlockSpec((rows, 1), lambda r, c: (r, 0)),
            ],
            out_specs=pl.BlockSpec((rows, classes), lambda r, c: (r, 0)),
            scratch_shapes=[pltpu.VMEM((own_tiles + halo_tiles, rows, classes), jnp.bfloat16)],
        ),
        compiler_params=pltpu.CompilerParams(
            dimension_semantics=("arbitrary",), vmem_limit_bytes=24 << 20
        ),
        cost_estimate=pl.CostEstimate(
            flops=2 * node_count * per_row * rows * classes,
            bytes_accessed=2 * (tile_weights.size + 2 * prior_labels.size),
            transcendentals=0,
        ),
    )(
        tile_cols,
        tile_weights,
        prior_labels.reshape(own_tiles, rows, classes),
        halo_labels.reshape(halo_tiles, rows, classes),
        seed_class[:, None],
    )


def on_device(
    prior_labels,
    label_class,
    labeled,
    features,
    tile_cols,
    tile_weights,
    halo_owner,
    halo_local,
    batch_owner,
    batch_local,
    w_in,
    w_out,
):
    devices = lax.axis_size("dev")
    chips = devices // 2
    me = lax.axis_index("dev")
    chip, core = me // 2, lax.rem(me, 2)
    swap = [(i, i ^ 1) for i in range(devices)]

    classes = prior_labels.shape[1]
    feat_width = features.shape[1]
    hidden_units = w_in.shape[0]
    unit_block = hidden_units // devices
    halo_count = halo_owner.shape[0]
    batch_count = batch_owner.shape[0]
    halo_capacity = 2 * halo_count // devices
    batch_capacity = 2 * batch_count // devices
    slots = devices * batch_capacity

    halo_slot = slot_of(halo_owner[:, 0], halo_capacity)
    batch_slot = slot_of(batch_owner[:, 0], batch_capacity)
    asked = jnp.concatenate(
        [
            request_table(halo_slot, halo_local, halo_capacity, devices),
            request_table(batch_slot, batch_local, batch_capacity, devices),
        ],
        axis=1,
    )
    wanted = lax.all_to_all(asked, "dev", split_axis=0, concat_axis=0, tiled=True)
    halo_wanted = jnp.maximum(wanted[:, :halo_capacity], 0).reshape(-1)
    batch_asked = wanted[:, halo_capacity:].reshape(-1)
    batch_wanted = jnp.maximum(batch_asked, 0)
    halo_served, batch_wanted = lax.optimization_barrier(
        (prior_labels[halo_wanted], batch_wanted)
    )
    halo_back = lax.all_to_all(
        halo_served.reshape(devices, halo_capacity, classes),
        "dev",
        split_axis=0,
        concat_axis=0,
        tiled=True,
    )

    bits = chips.bit_length() - 1
    order = [sum(((p >> (bits - 1 - k)) & 1) << k for k in range(bits)) for p in range(chips)]
    block = 2 * jnp.bitwise_xor(jnp.array(order, jnp.int32), chip) + core
    w_in_half = w_in.reshape(devices, unit_block, feat_width)[block].reshape(-1, feat_width)
    w_out_half = w_out.reshape(devices, unit_block, classes)[block].reshape(-1, classes)

    def both_cores(own):
        return jnp.concatenate([own, lax.ppermute(own, "dev", swap)], axis=0)

    x_own = features[batch_wanted]
    x = both_cores(x_own)
    hidden = jnp.tanh(contract_cols(x, w_in_half)).astype(jnp.bfloat16)
    partial = jnp.dot(hidden, w_out_half, preferred_element_type=jnp.float32)
    logits = partial[:slots] + lax.ppermute(partial[slots:], "dev", swap)

    halo_labels = halo_back.reshape(devices * halo_capacity, classes)[halo_slot]
    seed_class = jnp.where(labeled == 1, label_class, -1)
    propagated = propagate(tile_cols, tile_weights, prior_labels, halo_labels, seed_class)

    log_z = jnp.log(propagated[batch_wanted].astype(jnp.float32))
    target = log_z - jnp.mean(log_z, axis=1, keepdims=True)
    differ = logits - target
    slot_error = 0.5 * jnp.mean(differ * differ, axis=1)
    scaled = differ / math.sqrt(batch_count * devices)
    residue_own = jnp.where((batch_asked >= 0)[:, None], scaled, 0.0).astype(jnp.bfloat16)
    residue = both_cores(residue_own)

    hidden_near, hidden_far = jnp.split(hidden, 2, axis=1)
    w_out_near, w_out_far = jnp.split(w_out_half, 2, axis=0)

    def back_of(hidden, w_out_part, residue):
        hidden_wide = hidden.astype(jnp.float32)
        gate = 1.0 - hidden_wide * hidden_wide
        return (contract_cols(residue, w_out_part) * gate).astype(jnp.bfloat16)

    def cross(part, bit):
        return lax.ppermute(part, "dev", [(i, i ^ (2 << bit)) for i in range(devices)])

    def halves(total):
        return total[: total.shape[0] // 2], total[total.shape[0] // 2 :]

    def finish(near, far, stages):
        for bit, kind in stages:
            total = near + cross(far.astype(kind), bit).astype(jnp.float32)
            if total.shape[0] > unit_block:
                near, far = halves(total)
        return total

    bf16, f32 = jnp.bfloat16, jnp.float32
    rest = [(bit, f32) for bit in range(2, bits)]
    x_first, x_second = jnp.split(x, 2, axis=1)
    fence = lax.optimization_barrier

    out_far, residue_far = fence((contract_rows(hidden_far, residue).astype(bf16), residue))
    back_far = back_of(hidden_far, w_out_far, residue_far)
    far_near, far_far = halves(contract_rows(back_far, x_first))
    far_far, back_far = fence((far_far.astype(bf16), back_far))
    second_far, residue_near, slot_error = fence(
        (contract_rows(back_far, x_second).astype(bf16), residue_far, slot_error)
    )
    back_near = back_of(hidden_near, w_out_near, residue_near)
    near_near, near_far = halves(contract_rows(back_near, x_first))
    near_far, back_near, residue_near = fence((near_far.astype(bf16), back_near, residue_near))
    out_near = fence(contract_rows(hidden_near, residue_near))
    second_near = fence(contract_rows(back_near, x_second))

    grad_out = finish(out_near, out_far, [(0, bf16), (1, bf16)] + rest)
    in_second = finish(second_near, second_far, [(0, bf16), (1, bf16)] + rest)
    in_first = finish(
        near_near + cross(near_far, 1).astype(f32),
        far_near + cross(far_far, 1).astype(f32),
        [(0, bf16)] + rest,
    )
    grad_in = jnp.concatenate([in_first, in_second], axis=1)

    error_back = lax.all_to_all(
        slot_error.reshape(devices, batch_capacity),
        "dev",
        split_axis=0,
        concat_axis=0,
        tiled=True,
    ).reshape(-1)
    mine = batch_slot[:, None] == jnp.arange(slots, dtype=jnp.int32)[None, :]
    row_error = jnp.sum(jnp.where(mine, error_back[None, :], 0.0), axis=1)
    return (propagated, row_error, grad_in, grad_out)


def solution(mesh):
    in_specs = (
        P("dev", None),
        P("dev"),
        P("dev"),
        P("dev", None),
        P("dev", None),
        P("dev", None, None, None),
        P("dev", None),
        P("dev"),
        P("dev", None),
        P("dev"),
        P(),
        P(),
    )
    out_specs = (P("dev", None), P("dev"), P("dev", None), P("dev", None))
    return jax.shard_map(
        on_device, mesh=mesh, in_specs=in_specs, out_specs=out_specs, check_vma=False
    )
```
